32 devices in a mesh: grp: 8 (over y, x, core), eig: 4 (over z).
Axes of the slice: x: 2, y: 2, z: 4, core: 2. Of those that a mesh axis runs over, the one named last changes fastest.
Arguments:
- features: bfloat16 [32768, 128], P(('grp', 'eig')), may hold values from -6 to 6
- eigvals: float32 [32768], P(('grp', 'eig')), may hold values from 0 to 2, as said below
- graph_ids: int32 [8, 4096], P('grp', 'eig'), may hold values from 0 to 2, never falling along the last dimension, each value on 1 to 2048 neighbouring positions
- out_cot: bfloat16 [32768, 128], P(('grp', 'eig')), may hold values from -6 to 6
- bases_cot: float32 [32768, 4], P(('grp', 'eig')), may hold values from -6 to 6
- row_weights: bfloat16 [128, 896], replicated
- down_weights: bfloat16 [256, 128], replicated, may hold values from -0.375 to 0.375
- vectors: float32 [12, 128], replicated
- row_master: float32 [128, 896], P('grp')
- row_first: float32 [128, 896], P('grp')
- row_second: float32 [128, 896], P('grp')
- down_master: float32 [256, 128], P('grp'), may hold values from -0.375 to 0.375
- down_first: float32 [256, 128], P('grp'), may hold values from -64 to 64
- down_second: float32 [256, 128], P('grp'), may hold values from 8.192 to 32.768
- vec_first: float32 [12, 128], replicated, may hold values from -128 to 128
- vec_second: float32 [12, 128], replicated, may hold values from 32.768 to 131.072
Outputs:
- block_out: bfloat16 [32768, 128], P(('grp', 'eig'))
- bases: float32 [32768, 4], P(('grp', 'eig'))
- grad_features: float32 [32768, 128], P(('grp', 'eig'))
- row_master_new: float32 [128, 896], P('grp')
- row_first_new: float32 [128, 896], P('grp')
- row_second_new: float32 [128, 896], P('grp')
- down_master_new: float32 [256, 128], P('grp')
- down_first_new: float32 [256, 128], P('grp')
- down_second_new: float32 [256, 128], P('grp')
- vec_master_new: float32 [12, 128], replicated
- vec_first_new: float32 [12, 128], replicated
- vec_second_new: float32 [12, 128], replicated
The draws below stay inside these ranges and needn't reach their ends.
Inputs may be any that keep to these rules, and one draw needn't show every extreme that they name: `eigvals`: each eigenvalue is a multiple of 1/16; equal values recur.
All inputs are finite; a program needn't handle non-finite values.
Results may differ from the reference program's by a relative error of at most 0.015.
Values may be sent and summed in bfloat16 or wider, within the bound.
A program may use at most 256 MiB of HBM per device.

```python
import math
import jax
import jax.numpy as jnp
import numpy as np
from jax import lax

D = 128
FF = 256
HEADS = 4
BASES = 4
GRAPHS = 3
STEP = 5
GROUP_TOK = 4096
TOKENS = 32768
MOST = 2048
RW = 896
VEC = 12
N_GRP = 8


def block_values(enc_value, query_value, value_value, out_value, up_value):
    column = jnp.arange(RW)
    return jnp.where(column < D, enc_value, jnp.where(column < 3 * D, query_value, jnp.where(column < 4 * D, value_value, jnp.where(column < 5 * D, out_value, up_value))))


def weight_scales():
    base_scale = D ** (-0.5)
    return block_values(base_scale, 1.4 * base_scale, base_scale, 6.0 * base_scale, base_scale)


def grad_scales():
    root_tokens = jnp.sqrt(jnp.float32(TOKENS))
    return root_tokens * block_values(0.7, 0.3, 0.3, 0.2, 0.5)


def draw_eigvals(key, part):
    levels = jax.random.randint(jax.random.fold_in(key, 11), (TOKENS,), 0, 33)
    return levels.astype(jnp.float32) * 0.0625


def draw_row_weights(key, part):
    noise = jax.random.normal(jax.random.fold_in(key, 12), (D, RW), jnp.float32)
    return (noise * weight_scales()[None, :]).astype(jnp.bfloat16)


def draw_row_master(key, part):
    noise = jax.random.normal(jax.random.fold_in(key, 13), (D, RW), jnp.float32)
    return noise * weight_scales()[None, :]


def draw_row_first(key, part):
    noise = jax.random.normal(jax.random.fold_in(key, 14), (D, RW), jnp.float32)
    return noise * 0.11 * grad_scales()[None, :]


def draw_row_second(key, part):
    factor = jnp.exp(jax.random.uniform(jax.random.fold_in(key, 15), (D, RW), jnp.float32, jnp.log(0.001), jnp.log(0.004)))
    scales = grad_scales()
    return factor * (scales * scales)[None, :]


def draw_vectors(key, part):
    row_index = jnp.arange(VEC)[:, None]
    noise = jax.random.normal(jax.random.fold_in(key, 16), (VEC, D), jnp.float32)
    gain_rows = (row_index == 0) | (row_index == 2)
    decoder_rows = row_index >= VEC - BASES
    return jnp.where(gain_rows, 1.0 + 0.25 * noise, jnp.where(decoder_rows, noise * D ** (-0.5), 0.3 * noise))


def block_scale(stream_key, shape, cuts, smallest, top_value):
    def one(axis_at, parts):
        heights = jax.random.uniform(jax.random.fold_in(jax.random.fold_in(stream_key, 6), axis_at), (parts,), jnp.float32, smallest / len(cuts), top_value / len(cuts))
        return jnp.repeat(jnp.exp(heights), shape[axis_at] // parts).reshape((-1,) + (1,) * (len(shape) - axis_at - 1))

    factor_of = one(*cuts[0])
    for cut in cuts[1:]:
        factor_of = factor_of * one(*cut)
    return factor_of


def profile(count, total, bound, lean):
    weights = [(1 << 20) // math.isqrt(standing ** lean) + 1 for standing in range(2, count + 1)]
    rest, holding = total - bound - (count - 1), [1] * (count - 1)
    while rest > 0:
        movable = [i for i in range(count - 1) if holding[i] < bound]
        mass, budget = sum([weights[i] for i in movable]), rest
        for i in movable:
            extra = min(bound - holding[i], max(1, budget * weights[i] // mass), rest)
            holding[i] = holding[i] + extra
            rest = rest - extra
    return np.array([bound] + holding)


def uneven(rng, amount, total, most, lean):
    if amount == 2:
        one = jax.random.randint(rng, (), max(1, total - most), min(most, total - 1) + 1)
        return jnp.stack([one, total - one])
    sizes = jnp.asarray(profile(amount, total, most, lean), jnp.int32)
    couples = (amount - 1) // 2
    source_of, sink = sizes[1:1 + 2 * couples:2], sizes[2:2 + 2 * couples:2]
    slack = jnp.minimum(source_of - 1, most - sink)
    moved = jax.random.randint(jax.random.fold_in(rng, 1), (couples,), 0, 1 << 20) % (slack + 1)
    sizes = sizes.at[1:1 + 2 * couples:2].set(source_of - moved).at[2:2 + 2 * couples:2].set(sink + moved)
    return sizes[jax.random.permutation(jax.random.fold_in(rng, 2), amount)]


def scatter_about(key, shape, width, bound, cuts=(), kind=jnp.bfloat16):
    values = jax.random.normal(key, shape, jnp.float32) * width
    if len(cuts) > 0:
        values = block_scale(key, shape, cuts, -0.22, 0.18) * values
    return jnp.clip(values, min=-bound, max=bound).astype(kind)


def setup_inputs(seed: int = 0) -> dict:
    key_of = jax.random.split(jax.random.key(seed), 17)
    return {
        "features": scatter_about(key_of[0], (TOKENS, D), 1.0, 6.0, ((0, 32),)),
        "eigvals": draw_eigvals(jax.random.fold_in(key_of[16], 71), 0),
        "graph_ids": jax.vmap(lambda own: jnp.searchsorted(jnp.cumsum(uneven(own, GRAPHS, GROUP_TOK, MOST, 2)), jnp.arange(GROUP_TOK), side="right"))(jax.random.split(key_of[2], N_GRP)).reshape((N_GRP, GROUP_TOK)).astype(jnp.int32),
        "out_cot": scatter_about(key_of[3], (TOKENS, D), 1.0, 6.0, ((0, 32),)),
        "bases_cot": scatter_about(key_of[4], (TOKENS, BASES), 1.0, 6.0, ((0, 32),), jnp.float32),
        "row_weights": draw_row_weights(jax.random.fold_in(key_of[16], 71), 0),
        "down_weights": scatter_about(key_of[6], (FF, D), FF ** -0.5, 0.375),
        "vectors": draw_vectors(jax.random.fold_in(key_of[16], 71), 0),
        "row_master": draw_row_master(jax.random.fold_in(key_of[16], 71), 0),
        "row_first": draw_row_first(jax.random.fold_in(key_of[16], 71), 0),
        "row_second": draw_row_second(jax.random.fold_in(key_of[16], 71), 0),
        "down_master": scatter_about(key_of[11], (FF, D), FF ** -0.5, 0.375, ((0, 8),), jnp.float32),
        "down_first": scatter_about(key_of[12], (FF, D), (0.055 * TOKENS ** 0.5), 64.0, ((0, 8),), jnp.float32),
        "down_second": jnp.clip(jnp.exp(math.log(32.768) - 1.3862944 * jax.random.uniform(key_of[13], (FF, D), jnp.float32) ** block_scale(key_of[13], (FF, D), ((0, 8),), -0.2, 0.2)), 8.192, 32.768),
        "vec_first": scatter_about(key_of[14], (VEC, D), (0.11 * TOKENS ** 0.5), 128.0, (), jnp.float32),
        "vec_second": jnp.clip(jnp.exp(jax.random.uniform(key_of[15], (VEC, D), jnp.float32, math.log(32.768), math.log(131.072))), 32.768, 131.072),
    }


@jax.custom_vjp
def low(v):
    return lax.optimization_barrier(v.astype(jnp.bfloat16)).astype(jnp.float32)

@jax.custom_vjp
def low_back(v):
    return v

def low_keep(v):
    return (low(v), None)

def low_pass(kept, grad):
    return (grad,)

def back_keep(v):
    return (v, None)

def back_low(kept, grad):
    return (low(grad),)
low.defvjp(low_keep, low_pass)
low_back.defvjp(back_keep, back_low)
HIGH = lax.Precision.HIGHEST
NEG_FILL = -1e+30
NORM_EPS = 1e-05
BETA_ONE = 0.9
BETA_TWO = 0.999
EPSILON = 1e-08
DECAY = 0.01
RATE = 0.5

def matmul(left, right):
    return jnp.dot(left, right, precision=HIGH)

def encode(lams):
    index = jnp.arange(D // 2, dtype=jnp.float32)
    divisor = jnp.exp(index * (-2.0 * math.log(10000.0) / D))
    angles = lams[:, None] * 100.0 * divisor[None, :]
    return jnp.concatenate([jnp.sin(angles), jnp.cos(angles)], axis=1)

def layer_norm(values, gain, shift):
    center = values - lax.optimization_barrier(jnp.mean(values, axis=-1, keepdims=True))
    spread = lax.optimization_barrier(jnp.mean(center * center, axis=-1, keepdims=True))
    return center * lax.rsqrt(spread + NORM_EPS) * gain + shift

def attend(query, keys, values, labels):
    head_dim = D // HEADS
    block_rows = min(512, GROUP_TOK)
    key_heads = keys.reshape(GROUP_TOK, HEADS, head_dim)
    value_heads = values.reshape(GROUP_TOK, HEADS, head_dim)

    @jax.checkpoint
    def one_block(item):
        query_block, label_block = item
        scores = low_back(jnp.einsum('qhd,khd->hqk', query_block, key_heads, precision=HIGH))
        allowed = (label_block[:, None] == labels[None, :])[None]
        scores = jnp.where(allowed, scores, NEG_FILL)
        peak = lax.optimization_barrier(jnp.max(scores, axis=-1, keepdims=True))
        expos = jnp.exp(scores - peak)
        probs = low(expos / lax.optimization_barrier(jnp.sum(expos, axis=-1, keepdims=True)))
        return jnp.einsum('hqk,khd->qhd', probs, value_heads, precision=HIGH).reshape(block_rows, D)
    blocks = lax.map(one_block, (query.reshape(-1, block_rows, HEADS, head_dim), labels.reshape(-1, block_rows)))
    return blocks.reshape(GROUP_TOK, D)

def block(inputs, encoded, labels, row_all, down_all, vec_all):
    up_rows = FF // D
    w_enc = row_all[:, 0:D]
    w_qkv = row_all[:, D:4 * D]
    w_out = row_all[:, 4 * D:5 * D]
    w_up = row_all[:, 5 * D:]
    scale = 1.0 / math.sqrt(D // HEADS)
    hidden = inputs + low_back(matmul(low(encoded), w_enc))
    a_one = low(layer_norm(hidden, vec_all[0], vec_all[1]))
    qkv = matmul(a_one, w_qkv)
    query = low(low_back(qkv[:, 0:D]) * scale)
    keys = low(low_back(qkv[:, D:2 * D]))
    values = low(low_back(qkv[:, 2 * D:3 * D]))
    att = low(low_back(attend(query, keys, values, labels)))
    hidden_two = hidden + low_back(matmul(att, w_out) + vec_all[5 + up_rows])
    a_two = low(layer_norm(hidden_two, vec_all[2], vec_all[3]))
    up_pre = low_back(matmul(a_two, w_up) + vec_all[4:4 + up_rows].reshape(FF))
    gelled = low(jax.nn.gelu(up_pre, approximate=True))
    hidden_three = hidden_two + low_back(matmul(gelled, down_all) + vec_all[4 + up_rows])
    decoded = matmul(low(hidden_three), vec_all[6 + up_rows:].T)
    return (hidden_three, decoded)

def adamw(master, first, second, grad):
    first_new = BETA_ONE * first + (1.0 - BETA_ONE) * grad
    second_new = BETA_TWO * second + (1.0 - BETA_TWO) * grad * grad
    first_hat = first_new / (1.0 - BETA_ONE ** STEP)
    second_hat = second_new / (1.0 - BETA_TWO ** STEP)
    master_new = master - RATE * (first_hat / (jnp.sqrt(second_hat) + EPSILON) + DECAY * master)
    return (master_new, first_new, second_new)

def reference(features, eigvals, graph_ids, out_cot, bases_cot, row_weights, down_weights, vectors, row_master, row_first, row_second, down_master, down_first, down_second, vec_first, vec_second):
    rows_float = row_weights.astype(jnp.float32)
    down_float = down_weights.astype(jnp.float32)
    items = (features.astype(jnp.float32).reshape(N_GRP, GROUP_TOK, D), eigvals.reshape(N_GRP, GROUP_TOK), graph_ids, out_cot.astype(jnp.float32).reshape(N_GRP, GROUP_TOK, D), bases_cot.reshape(N_GRP, GROUP_TOK, BASES))
    start_totals = (jnp.zeros((D, RW), jnp.float32), jnp.zeros((FF, D), jnp.float32), jnp.zeros((VEC, D), jnp.float32))

    def one_group(totals, item):
        group_feats, group_lams, labels, group_cot, group_bases_cot = item
        encoded = encode(group_lams)

        def forward(inputs, row_all, down_all, vec_all):
            return block(inputs, encoded, labels, row_all, down_all, vec_all)
        (group_out, group_bases), backward = jax.vjp(forward, group_feats, rows_float, down_float, vectors)
        grad_in, grad_rows, grad_down, grad_vec = backward((group_cot, group_bases_cot))
        totals = (totals[0] + grad_rows, totals[1] + grad_down, totals[2] + grad_vec)
        return (totals, (group_out.astype(jnp.bfloat16), group_bases, grad_in))
    totals, (outputs, decoded, grad_inputs) = lax.scan(one_group, start_totals, items)
    row_new = adamw(row_master, row_first, row_second, totals[0])
    down_new = adamw(down_master, down_first, down_second, totals[1])
    vec_new = adamw(vectors, vec_first, vec_second, totals[2])
    return (outputs.reshape(TOKENS, D), decoded.reshape(TOKENS, BASES), grad_inputs.reshape(TOKENS, D), row_new[0], row_new[1], row_new[2], down_new[0], down_new[1], down_new[2], vec_new[0], vec_new[1], vec_new[2])
```

```python
import functools
import math

import jax
import jax.numpy as jnp
import numpy as np
from jax import lax
from jax.experimental import pallas as pl
from jax.experimental.pallas import tpu as pltpu
from jax.sharding import PartitionSpec as P

HEADS = 4
STEP = 5
GRAPHS = 3
LEVELS = 33

NORM_EPS = 1e-05
BETA_ONE = 0.9
BETA_TWO = 0.999
EPSILON = 1e-08
DECAY = 0.01
RATE = 0.5

BF = jnp.bfloat16
F32 = jnp.float32
LOG2E = math.log2(math.e)
BLOCKED = -1e30
SAFE_RANGE = 80.0
QB = 256
CHUNK = 1152
EIG_ROWS = 40
CODE_ROWS = 48
VMEM = pl.BlockSpec(memory_space=pltpu.VMEM)
ANY = pl.BlockSpec(memory_space=pl.ANY)
MESH = pl.DeviceIdType.MESH


def encode_table(width):
    lams = (np.arange(EIG_ROWS) / 16.0).astype(np.float32)
    index = np.arange(width // 2, dtype=np.float32)
    divisor = np.exp(index * np.float32(-2.0 * math.log(10000.0) / width)).astype(np.float32)
    angles = (lams[:, None] * np.float32(100.0)) * divisor[None, :]
    table = np.concatenate([np.sin(angles.astype(np.float64)), np.cos(angles.astype(np.float64))], 1)
    table[LEVELS:] = 0.0
    return table.astype(np.float32)


def adamw(master, first, second, grad):
    first_new = BETA_ONE * first + (1.0 - BETA_ONE) * grad
    second_new = BETA_TWO * second + (1.0 - BETA_TWO) * grad * grad
    first_hat = first_new / (1.0 - BETA_ONE**STEP)
    second_hat = second_new / (1.0 - BETA_TWO**STEP)
    master_new = master - RATE * (first_hat / (jnp.sqrt(second_hat) + EPSILON) + DECAY * master)
    return (master_new, first_new, second_new)


def nn(left, right):
    return lax.dot_general(left, right, (((1,), (0,)), ((), ())), preferred_element_type=F32)


def nt(left, right):
    return lax.dot_general(left, right, (((1,), (1,)), ((), ())), preferred_element_type=F32)


def tn(left, right):
    return lax.dot_general(left, right, (((0,), (0,)), ((), ())), preferred_element_type=F32)


def split(values):
    high = values.astype(BF)
    return high, (values - high.astype(F32)).astype(BF)


def iota(shape, dim):
    return lax.broadcasted_iota(jnp.int32, shape, dim)


def one_hot_rows(code):
    label = jnp.floor(code * (1.0 / 64.0))
    level = code - 64.0 * label
    row = iota((CODE_ROWS, code.shape[1]), 0).astype(F32)
    hit = jnp.where(row < EIG_ROWS, level, label + EIG_ROWS) == row
    return jnp.where(hit, 1.0, 0.0).astype(BF)


def lane_sums(values):
    high, low = split(values)
    ones = jnp.ones((8, values.shape[1]), BF)
    return nt(ones, high) + nt(ones, low)


def norm_stats(values):
    center = values - jnp.mean(values, axis=0, keepdims=True)
    spread = jnp.mean(center * center, axis=0, keepdims=True)
    rstd = lax.rsqrt(spread + NORM_EPS)
    return center * rstd, rstd


def norm_back(hat, rstd, gain, grad):
    scaled = grad * gain
    first = jnp.mean(scaled, axis=0, keepdims=True)
    second = jnp.mean(scaled * hat, axis=0, keepdims=True)
    return rstd * (scaled - first - hat * second)


def columns_of(vec):
    count = vec.shape[0]
    padded = jnp.concatenate([vec, jnp.zeros((vec.shape[1] - count, vec.shape[1]), F32)], axis=0)
    return padded.T


def gather_kernel(n, reach, feat, eig, labels, gfeat, gcode, code, send, recv, csend, crecv, lsem):
    me = lax.axis_index("eig")
    barrier = pltpu.get_barrier_semaphore()
    steps = [d for r in range(1, reach + 1) for d in (-r, r)]
    count = jnp.int32(0)
    for d in steps:
        inside = (me + d >= 0) & (me + d < n)
        count = count + jnp.where(inside, 1, 0)

        @pl.when(inside)
        def _():
            pl.semaphore_signal(barrier, inc=1, device_id={"eig": me + d}, device_id_type=MESH)

    code[...] = labels[...].astype(F32) * 64.0 + jnp.round(eig[...] * 16.0)
    own = pltpu.make_async_copy(feat, gfeat.at[me], lsem.at[0])
    own.start()
    own_code = pltpu.make_async_copy(code, gcode.at[me], lsem.at[1])
    own_code.start()
    pl.semaphore_wait(barrier, count)

    def copies(i, d, slot, peer):
        return (
            pltpu.make_async_remote_copy(
                feat, gfeat.at[slot], send.at[i], recv.at[i],
                device_id={"eig": peer}, device_id_type=MESH,
            ),
            pltpu.make_async_remote_copy(
                code, gcode.at[slot], csend.at[i], crecv.at[i],
                device_id={"eig": peer}, device_id_type=MESH,
            ),
        )

    for i, d in enumerate(steps):

        @pl.when((me + d >= 0) & (me + d < n))
        def _():
            for copy in copies(i, d, me, me + d):
                copy.start()

    for i, d in enumerate(steps):

        @pl.when((me - d >= 0) & (me - d < n))
        def _():
            for copy in copies(i, d, me - d, me - d):
                copy.wait_recv()

    for i, d in enumerate(steps):

        @pl.when((me + d >= 0) & (me + d < n))
        def _():
            for copy in copies(i, d, me, me + d):
                copy.wait_send()

    own.wait()
    own_code.wait()


def layer_kernel(
    n, reach, grp_count, store_e, slots, per_slot,
    gfeat, gcode, out_cot, bcot, w, down, vec, table,
    out, bases, da_part, dh2_out, grads,
    kx, vx, k_t, v_t, a1_t, q_rows, lab_rows, q_blocks, m_rows, e_buf,
    o_acc, dq_acc, d_rows, dk, dv, plan,
):
    width = out_cot.shape[1]
    tok = out_cot.shape[0]
    hidden = down.shape[0]
    up_rows = hidden // width
    dim = width // HEADS
    scale = 1.0 / math.sqrt(dim)
    me = lax.axis_index("eig")
    first_valid = jnp.maximum(me - reach, 0)
    end_valid = jnp.minimum(me + reach + 1, n)
    base = me * tok
    wide = HEADS * QB

    w_enc = w[:, 0:width]
    w_q = w[:, width : 2 * width]
    w_k = w[:, 2 * width : 3 * width]
    w_v = w[:, 3 * width : 4 * width]
    w_out = w[:, 4 * width : 5 * width]
    w_up = w[:, 5 * width :]
    flipped = w[...].astype(F32).T.astype(BF)
    enc_t = flipped[0:width]
    wk_t = flipped[2 * width : 3 * width]
    wv_t = flipped[3 * width : 4 * width]
    out_t = flipped[4 * width : 5 * width]
    up_t = flipped[5 * width :]
    down_t = down[...].astype(F32).T.astype(BF)
    eye = jnp.where(iota((width, width), 0) == iota((width, width), 1), 1.0, 0.0).astype(BF)
    cols = columns_of(vec[...])

    starts = [first_valid * tok] * (GRAPHS + 1)
    for t in range(n):
        inside = (t >= first_valid) & (t < end_valid)
        label = jnp.floor(gcode[t] * (1.0 / 64.0))
        for g in range(GRAPHS):
            found = jnp.sum(jnp.where(label <= g, 1, 0))
            starts[g + 1] = starts[g + 1] + jnp.where(inside, found, 0)

    count = jnp.int32(0)
    low_key = jnp.int32(n * tok)
    high_key = jnp.int32(0)
    for g in range(GRAPHS):
        row_start = jnp.clip(starts[g] - base, 0, tok)
        row_end = jnp.clip(starts[g + 1] - base, 0, tok)
        q_start = (row_start // 128) * 128
        blocks = jnp.where(row_end > row_start, (row_end - q_start + QB - 1) // QB, 0)
        k_start = (starts[g] // 128) * 128
        chunks = (starts[g + 1] - k_start + CHUNK - 1) // CHUNK
        k_start = jnp.minimum(k_start, end_valid * tok - chunks * CHUNK)
        some = blocks > 0
        low_key = jnp.where(some, jnp.minimum(low_key, k_start), low_key)
        high_key = jnp.where(some, jnp.maximum(high_key, k_start + chunks * CHUNK), high_key)

        def note(b, at):
            plan[0, at] = g
            plan[1, at] = q_start + b * QB
            plan[2, at] = k_start
            plan[3, at] = chunks
            return at + 1

        count = lax.fori_loop(0, blocks, note, count)

    first_shard = low_key // tok
    end_shard = (high_key + tok - 1) // tok

    spread_rows = jnp.concatenate(
        [
            table[...],
            jnp.where(
                (iota((CODE_ROWS, 128), 0) - EIG_ROWS == iota((CODE_ROWS, 128), 1))
                & (iota((CODE_ROWS, 128), 0) >= EIG_ROWS),
                1.0, 0.0,
            ).astype(BF),
        ],
        axis=1,
    )
    gain_row = vec[0:1, :]
    shift_row = vec[1:2, :]
    vx[:, width:] = jnp.where(iota((vx.shape[0], 128), 1) < 2 * HEADS, 1.0, 0.0).astype(BF)
    v_t[width:, :] = jnp.ones((16, v_t.shape[1]), BF)
    lab_rows[...] = jnp.zeros_like(lab_rows)
    q_rows[...] = jnp.zeros_like(q_rows)

    def shard(t, biggest):
        rows = pl.ds(pl.multiple_of(t * tok, 128), tok)
        hot = one_hot_rows(gcode[t])
        spread = tn(hot, spread_rows)
        enc = spread[:, :width].astype(BF)
        lab = spread[:, width:].astype(BF)
        h = gfeat[t].astype(F32) + nn(enc, w_enc)
        center = h - jnp.mean(h, axis=1, keepdims=True)
        var = jnp.mean(center * center, axis=1, keepdims=True)
        a1 = (center * lax.rsqrt(var + NORM_EPS) * gain_row + shift_row).astype(BF)
        keys = nn(a1, w_k).astype(BF)
        kx[rows, 0:width] = keys
        kx[rows, width:] = lab
        vx[rows, 0:width] = nn(a1, w_v).astype(BF)
        k_t[:, rows] = nt(wk_t, a1).astype(BF)
        v_t[0:width, rows] = nt(wv_t, a1).astype(BF)
        a1_t[:, rows] = nt(eye, a1).astype(BF)

        @pl.when(t == me)
        def _():
            q_rows[0:tok, :] = (nn(a1, w_q) * scale).astype(BF)
            lab_rows[0:tok, :] = lab

        head_of = jnp.where(
            iota((width, 128), 0) // dim == iota((width, 128), 1), 1.0, 0.0
        ).astype(BF)
        wide_keys = keys.astype(F32)
        norms = nn((wide_keys * wide_keys).astype(BF), head_of)
        return jnp.maximum(biggest, jnp.max(norms))

    key_norm = lax.fori_loop(first_shard, end_shard, shard, jnp.float32(0.0))
    head_of = jnp.where(
        iota((width, 128), 0) // dim == iota((width, 128), 1), 1.0, 0.0
    ).astype(BF)
    wide_q = q_rows[0:tok, :].astype(F32)
    query_norm = jnp.max(nn((wide_q * wide_q).astype(BF), head_of))
    bound = (SAFE_RANGE / LOG2E / 1.02) ** 2
    unsafe = jnp.logical_not(key_norm * query_norm < bound)

    o_acc[...] = jnp.zeros_like(o_acc)
    dq_acc[...] = jnp.zeros_like(dq_acc)
    dk[...] = jnp.zeros_like(dk)
    dv[...] = jnp.zeros_like(dv)

    lane = iota((1, 2 * width), 1)
    head_lane = iota((1, width), 1) // dim

    def fill(slot):
        g = plan[0, slot]
        rows = pl.ds(pl.multiple_of(plan[1, slot], 128), QB)
        q = q_rows[rows, :]
        lab = lab_rows[rows, :].astype(F32)
        kind = iota((QB, 128), 1)
        block = jnp.where(
            kind < GRAPHS + 1,
            jnp.where((kind == g) & (lab > 0.5), 0.0, BLOCKED), 0.0,
        ).astype(BF)
        for head in range(HEADS):
            at = slice(head * QB, (head + 1) * QB)
            q_blocks[slot, at, 0:width] = jnp.where(head_lane == head, q, jnp.zeros_like(q))
            q_blocks[slot, at, width:] = block
        m_rows[slot] = jnp.zeros((8, wide), F32)

        @pl.when(unsafe)
        def _():
            def scan(c, top):
                keys = pl.ds(pl.multiple_of(plan[2, slot] + c * CHUNK, 128), CHUNK)
                scores = nt(kx[keys, :], q_blocks[slot]) * LOG2E
                return jnp.maximum(top, jnp.max(scores, axis=0, keepdims=True))

            top = lax.fori_loop(0, plan[3, slot], scan, jnp.full((1, wide), -1e38, F32))
            top = jnp.where(top < -1e28, 0.0, top)
            m_rows[slot] = jnp.broadcast_to(top, (8, wide))

    def make_e(slot, keys):
        scores = nt(kx[keys, :], q_blocks[slot])
        return jnp.exp2(scores * LOG2E - m_rows[slot, 0:1, :]).astype(BF)

    def forward(slot, carry):
        fill(slot)

        def chunk(c, inner):
            keys = pl.ds(pl.multiple_of(plan[2, slot] + c * CHUNK, 128), CHUNK)
            e = make_e(slot, keys)
            if store_e:
                e_buf[slot * per_slot + c] = e
            r = nn(v_t[:, keys], e)
            cols_at = pl.ds(pl.multiple_of(plan[1, slot], 128), QB)
            for head in range(HEADS):
                at = slice(head * QB, (head + 1) * QB)
                o_acc[head * dim : (head + 1) * dim, cols_at] += r[head * dim : (head + 1) * dim, at]
                o_acc[width + 8 * head : width + 8 * head + 8, cols_at] += r[width : width + 8, at]
            return inner

        return lax.fori_loop(0, plan[3, slot], chunk, carry)

    lax.fori_loop(0, count, forward, jnp.int32(0))

    share = width // grp_count
    down_share = hidden // grp_count

    def keep_rows(offset, grad):
        for g in range(grp_count):
            grads[g, :, offset : offset + grad.shape[1]] = grad[g * share : (g + 1) * share]

    hot = one_hot_rows(gcode[me])
    enc_own = tn(table[...], hot).astype(BF)
    h = nt(eye, gfeat[me]) + nn(enc_t, enc_own)
    inv = [
        1.0 / o_acc[width + 8 * head : width + 8 * head + 1, 0:tok] for head in range(HEADS)
    ]
    att_f = jnp.concatenate(
        [o_acc[head * dim : (head + 1) * dim, 0:tok] * inv[head] for head in range(HEADS)], axis=0
    )
    att = att_f.astype(BF)
    bias_out = cols[:, 5 + up_rows : 6 + up_rows]
    bias_down = cols[:, 4 + up_rows : 5 + up_rows]
    bias_up = jnp.concatenate([cols[:, 4 + r : 5 + r] for r in range(up_rows)], axis=0)
    h2 = h + nn(out_t, att) + bias_out
    hat2, rstd2 = norm_stats(h2)
    gain2 = cols[:, 2:3]
    a2 = (hat2 * gain2 + cols[:, 3:4]).astype(BF)
    u = nn(up_t, a2) + bias_up
    root = math.sqrt(2.0 / math.pi)
    square = u * u
    wave = jnp.tanh(root * (u * (1.0 + 0.044715 * square)))
    gel = (0.5 * u * (1.0 + wave)).astype(BF)
    slope = 0.5 * (1.0 + wave) + 0.5 * u * (1.0 - wave * wave) * (
        root * (1.0 + 3.0 * 0.044715 * square)
    )
    h3 = h2 + nn(down_t, gel) + bias_down
    out_low = h3.astype(BF)
    out[...] = h3.T.astype(BF)
    dec = vec[6 + up_rows :, :]
    dec_count = dec.shape[0]
    dec_high, dec_low = split(dec)
    dec_high = dec_high.astype(F32)
    dec_low = dec_low.astype(F32)
    pair = nn(jnp.concatenate([dec_high, dec_low], axis=0).astype(BF), out_low)
    bases[...] = pair[0:dec_count] + pair[dec_count : 2 * dec_count]
    cot_high, cot_low = split(bcot[...])
    cot_high = cot_high.astype(F32)
    cot_low = cot_low.astype(F32)
    cots = jnp.concatenate([cot_high, cot_low, cot_high, jnp.zeros_like(cot_low)], axis=0).astype(BF)
    decs = jnp.concatenate([dec_high, dec_high, dec_low, jnp.zeros_like(dec_low)], axis=0).astype(BF)
    dh3 = nt(eye, out_cot[...]) + tn(decs, cots)
    grad_pair = nt(jnp.concatenate([cot_high, cot_low], axis=0).astype(BF), out_low)
    grad_dec = grad_pair[0:dec_count] + grad_pair[dec_count : 2 * dec_count]
    dy2 = dh3.astype(BF)
    ones = jnp.ones((8, tok), BF)

    @pl.when(count >= 0)
    def _():
        grad_down = nt(gel, dy2)
        for g in range(grp_count):
            for r in range(up_rows):
                begin = g * down_share + r * share
                offset = 4 * width + hidden + r * width
                grads[g, :, offset : offset + width] = grad_down[begin : begin + share]

    grad_bdown = nt(ones, dy2)
    du = (nn(down[...], dy2) * slope).astype(BF)

    @pl.when(count >= 0)
    def _():
        keep_rows(4 * width, nt(a2, du))

    grad_bup = nt(ones, du)
    da2 = nn(w_up, du)
    grad_gain2 = lane_sums(da2 * hat2)
    grad_shift2 = lane_sums(da2)
    dh2 = dh3 + norm_back(hat2, rstd2, gain2, da2)
    dh2_out[...] = dh2
    dy1 = dh2.astype(BF)

    @pl.when(count >= 0)
    def _():
        keep_rows(3 * width, nt(att, dy1))

    grad_bout = nt(ones, dy1)
    datt = nn(w_out, dy1).astype(BF).astype(F32)
    lead = []
    extra = []
    for head in range(HEADS):
        part = datt[head * dim : (head + 1) * dim]
        delta = jnp.sum(part * att_f[head * dim : (head + 1) * dim], axis=0, keepdims=True)
        lead.append(part * inv[head])
        delta_high, delta_low = split(-delta * inv[head])
        extra.append(delta_high.astype(F32))
        extra.append(delta_low.astype(F32))
    d_rows[0:tok, 0:width] = jnp.concatenate(lead, axis=0).T.astype(BF)
    extra.append(jnp.zeros((128 - 2 * HEADS, tok), F32))
    d_rows[0:tok, width:] = jnp.concatenate(extra, axis=0).T.astype(BF)
    d_rows[tok:, :] = jnp.zeros((d_rows.shape[0] - tok, 2 * width), BF)

    def backward(slot, carry):
        rows = pl.ds(pl.multiple_of(plan[1, slot], 128), QB)
        drow = d_rows[rows, :]
        pieces = []
        for head in range(HEADS):
            keep = ((lane < width) & (lane // dim == head)) | (
                (lane >= width) & ((lane - width) // 2 == head)
            )
            pieces.append(jnp.where(keep, drow, jnp.zeros_like(drow)))
        d_block = jnp.concatenate(pieces, axis=0)

        def chunk(c, inner):
            keys = pl.ds(pl.multiple_of(plan[2, slot] + c * CHUNK, 128), CHUNK)
            if store_e:
                e = e_buf[slot * per_slot + c]
            else:
                e = make_e(slot, keys)
            dp = nt(vx[keys, :], d_block)
            ds = e * dp.astype(BF)
            r = nn(k_t[:, keys], ds)
            cols_at = pl.ds(pl.multiple_of(plan[1, slot], 128), QB)
            for head in range(HEADS):
                at = slice(head * QB, (head + 1) * QB)
                dq_acc[head * dim : (head + 1) * dim, cols_at] += r[head * dim : (head + 1) * dim, at]
            dk[keys, :] += nn(ds, q_blocks[slot, :, 0:width])
            dv[keys, :] += nn(e, d_block[:, 0:width])
            return inner

        return lax.fori_loop(0, plan[3, slot], chunk, carry)

    lax.fori_loop(0, count, backward, jnp.int32(0))

    dq = (dq_acc[:, 0:tok] * scale).astype(BF)
    a1_own = a1_t[:, pl.ds(pl.multiple_of(base, 128), tok)]

    @pl.when(count >= 0)
    def _():
        keep_rows(0, nt(a1_own, dq))

    da_own = nn(w_q, dq)

    def finish(t, totals):
        rows = pl.ds(pl.multiple_of(t * tok, 128), tok)
        dkt = dk[rows, :].astype(BF)
        dvt = dv[rows, :].astype(BF)
        a1 = a1_t[:, rows]
        part = nt(w_k, dkt) + nt(w_v, dvt)
        part = part + jnp.where(t == me, da_own, 0.0)
        da_part[t] = part.astype(BF)
        return (totals[0] + nn(a1, dkt), totals[1] + nn(a1, dvt))

    zero = jnp.zeros((width, width), F32)
    grad_k, grad_v = lax.fori_loop(first_shard, end_shard, finish, (zero, zero))

    def blank(t, carry):
        @pl.when((t < first_shard) | (t >= end_shard))
        def _():
            da_part[t] = jnp.zeros((width, tok), BF)

        return carry

    lax.fori_loop(first_valid, end_valid, blank, jnp.int32(0))

    keep_rows(width, grad_k)
    keep_rows(2 * width, grad_v)
    packs = 16 // share
    grad_vec = jnp.concatenate(
        [jnp.zeros((2, width), F32), grad_gain2[0:1], grad_shift2[0:1]]
        + [grad_bup[0:1, r * width : (r + 1) * width] for r in range(up_rows)]
        + [grad_bdown[0:1], grad_bout[0:1], grad_dec]
        + [jnp.zeros((16 - vec.shape[0], width), F32)],
        axis=0,
    )
    for g in range(grp_count):
        for r in range(packs):
            offset = 4 * width + 2 * hidden + r * width
            grads[g, :, offset : offset + width] = grad_vec[r * share : (r + 1) * share]


def finish_kernel(
    n, reach, grp_count,
    da_part, da_own, feat, eig, labels, dh2, w, vec, table, grads,
    row_master, row_first, row_second, down_master, down_first, down_second, vec_first, vec_second,
    grad_features, row_m, row_f, row_s, down_m, down_f, down_s, vec_m, vec_f, vec_s,
    da_in, early_in, late_out, late_in, early_mid, early_mids, late_mid, late_mids,
    da_send, da_recv, es, er, ls, lr, ems, emr, lms, lmr,
):
    me = lax.axis_index("eig")
    grp = lax.axis_index("grp")
    width = feat.shape[1]
    hidden = down_master.shape[0] * grp_count
    up_rows = hidden // width
    share = width // grp_count
    packs = 16 // share
    steps = [d for r in range(1, reach + 1) for d in (-r, r)]

    barrier = pltpu.get_barrier_semaphore()
    for d in range(1, grp_count):
        pl.semaphore_signal(
            barrier, inc=1, device_id={"grp": lax.rem(grp + d, grp_count)}, device_id_type=MESH
        )
    for d in range(1, n):
        pl.semaphore_signal(
            barrier, inc=1, device_id={"eig": lax.rem(me + d, n)}, device_id_type=MESH
        )
    pl.semaphore_wait(barrier, grp_count - 1 + n - 1)

    def da_copy(i, shard, peer):
        return pltpu.make_async_remote_copy(
            da_part.at[shard], da_in.at[i], da_send.at[i], da_recv.at[i],
            device_id={"eig": peer}, device_id_type=MESH,
        )

    def plane(source, target, send, recv, d):
        peer = lax.rem(grp + d, grp_count)
        return pltpu.make_async_remote_copy(
            source.at[peer], target.at[d], send.at[d], recv.at[d],
            device_id={"grp": peer}, device_id_type=MESH,
        )

    def line(source, target, send, recv, d):
        peer = lax.rem(me + d, n)
        return pltpu.make_async_remote_copy(
            source, target.at[d], send.at[d], recv.at[d],
            device_id={"eig": peer}, device_id_type=MESH,
        )

    for i, d in enumerate(steps):

        @pl.when((me + d >= 0) & (me + d < n))
        def _():
            da_copy(i, me + d, me + d).start()

    for d in range(1, grp_count):
        plane(grads, early_in, es, er, d).start()

    code = labels[...].astype(F32) * 64.0 + jnp.round(eig[...] * 16.0)
    hot = one_hot_rows(code)
    enc = tn(table[...], hot).astype(BF)
    enc_t = w[:, 0:width].astype(F32).T.astype(BF)
    eye = jnp.where(iota((width, width), 0) == iota((width, width), 1), 1.0, 0.0).astype(BF)
    hat, rstd = norm_stats(nt(eye, feat[...]) + nn(enc_t, enc))
    gain = columns_of(vec[...])[:, 0:1]

    def in_order(own, slots, index, size):
        total = None
        for member in range(size):
            away = lax.rem(index - member + size, size)
            term = slots[away]
            total = term if total is None else total + term
        return total

    early_in[0] = grads[grp]
    for d in range(1, grp_count):
        plane(grads, early_in, es, er, d).wait_recv()
    early_mid[...] = in_order(None, early_in, grp, grp_count)
    early_mids[0] = early_mid[...]
    for d in range(1, n):
        line(early_mid, early_mids, ems, emr, d).start()

    da = da_own[0].astype(F32)
    for i, d in enumerate(steps):

        @pl.when((me - d >= 0) & (me - d < n))
        def _():
            da_copy(i, me - d, me - d).wait_recv()

        @pl.when((me - d < 0) | (me - d >= n))
        def _():
            da_in[i] = jnp.zeros_like(da_in[i])

    for i in range(len(steps)):
        da = da + da_in[i].astype(F32)
    grad_gain = lane_sums(da * hat)
    grad_shift = lane_sums(da)
    gf = dh2[...] + norm_back(hat, rstd, gain, da)
    grad_features[...] = gf.T
    grad_enc = nt(enc, gf.astype(BF))
    pair = jnp.concatenate([grad_gain[0:1], grad_shift[0:1]], axis=0)
    for g in range(grp_count):
        late_out[g, :, 0:width] = grad_enc[g * share : (g + 1) * share]
        late_out[g, 0:2, width:] = pair
        late_out[g, 2:, width:] = jnp.zeros((share - 2, width), F32)
    late_in[0] = late_out[grp]
    for d in range(1, grp_count):
        plane(late_out, late_in, ls, lr, d).start()
    for d in range(1, grp_count):
        plane(late_out, late_in, ls, lr, d).wait_recv()
    late_mid[...] = in_order(None, late_in, grp, grp_count)
    late_mids[0] = late_mid[...]
    for d in range(1, n):
        line(late_mid, late_mids, lms, lmr, d).start()

    for d in range(1, n):
        line(early_mid, early_mids, ems, emr, d).wait_recv()
    early = in_order(None, early_mids, me, n)
    body = width * 4 + hidden - width
    down_grad = jnp.concatenate(
        [
            early[:, 4 * width + hidden + r * width : 4 * width + hidden + (r + 1) * width]
            for r in range(up_rows)
        ],
        axis=0,
    )
    down_m[...], down_f[...], down_s[...] = adamw(
        down_master[...], down_first[...], down_second[...], down_grad
    )
    tail = slice(width, 5 * width + hidden)
    row_m[:, tail], row_f[:, tail], row_s[:, tail] = adamw(
        row_master[:, tail], row_first[:, tail], row_second[:, tail], early[:, 0 : 4 * width + hidden]
    )
    for d in range(1, n):
        line(late_mid, late_mids, lms, lmr, d).wait_recv()
    late = in_order(None, late_mids, me, n)
    head = slice(0, width)
    row_m[:, head], row_f[:, head], row_s[:, head] = adamw(
        row_master[:, head], row_first[:, head], row_second[:, head], late[:, 0:width]
    )
    offset = 4 * width + 2 * hidden
    vec_grad = jnp.concatenate(
        [early[:, offset + r * width : offset + (r + 1) * width] for r in range(packs)], axis=0
    )
    count = vec.shape[0]
    vec_grad = jnp.concatenate([late[0:2, width:], vec_grad[2:count]], axis=0)
    vec_m[...], vec_f[...], vec_s[...] = adamw(vec[...], vec_first[...], vec_second[...], vec_grad)

    for i, d in enumerate(steps):

        @pl.when((me + d >= 0) & (me + d < n))
        def _():
            da_copy(i, me + d, me + d).wait_send()

    for d in range(1, grp_count):
        plane(grads, early_in, es, er, d).wait_send()
        plane(late_out, late_in, ls, lr, d).wait_send()
    for d in range(1, n):
        line(early_mid, early_mids, ems, emr, d).wait_send()
        line(late_mid, late_mids, lms, lmr, d).wait_send()


def per_device(
    n,
    grp_count,
    features,
    eigvals,
    graph_ids,
    out_cot,
    bases_cot,
    row_weights,
    down_weights,
    vectors,
    row_master,
    row_first,
    row_second,
    down_master,
    down_first,
    down_second,
    vec_first,
    vec_second,
):
    tok, width = features.shape
    hidden = down_weights.shape[0]
    reach = n // 2
    total = n * tok
    most = total // 2
    eig_row = eigvals.reshape(1, tok)
    table = jnp.asarray(
        np.pad(encode_table(width), ((0, CODE_ROWS - EIG_ROWS), (0, 0))), BF
    )
    shape = jax.ShapeDtypeStruct
    dma = pltpu.SemaphoreType.DMA

    gfeat, gcode = pl.pallas_call(
        functools.partial(gather_kernel, n, reach),
        out_shape=[shape((n, tok, width), BF), shape((n, 1, tok), F32)],
        in_specs=[VMEM, VMEM, VMEM],
        out_specs=[ANY, ANY],
        scratch_shapes=[pltpu.VMEM((1, tok), F32)]
        + [dma((2 * reach,)) for _ in range(4)]
        + [dma((2,))],
        compiler_params=pltpu.CompilerParams(collective_id=0, has_side_effects=True),
        name="gather",
    )(features, eig_row, graph_ids)

    per_slot = (most + 127 + CHUNK - 1) // CHUNK
    slots = (tok + 2 * 127) // QB + GRAPHS
    store_e = total <= 4096
    padded = tok + QB
    share = width // grp_count
    lanes = 4 * width + 2 * hidden + width * (16 // share)
    e_shape = (slots * per_slot, CHUNK, HEADS * QB) if store_e else (1, 16, 128)
    out, bases, da_part, dh2, grads = pl.pallas_call(
        functools.partial(layer_kernel, n, reach, grp_count, store_e, slots, per_slot),
        out_shape=[
            shape((tok, width), BF),
            shape((bases_cot.shape[1], tok), F32),
            shape((n, width, tok), BF),
            shape((width, tok), F32),
            shape((grp_count, share, lanes), F32),
        ],
        in_specs=[VMEM] * 8,
        out_specs=[VMEM] * 5,
        scratch_shapes=[
            pltpu.VMEM((total, 2 * width), BF),
            pltpu.VMEM((total, 2 * width), BF),
            pltpu.VMEM((width, total), BF),
            pltpu.VMEM((width + 16, total), BF),
            pltpu.VMEM((width, total), BF),
            pltpu.VMEM((padded, width), BF),
            pltpu.VMEM((padded, 128), BF),
            pltpu.VMEM((slots, HEADS * QB, 2 * width), BF),
            pltpu.VMEM((slots, 8, HEADS * QB), F32),
            pltpu.VMEM(e_shape, BF),
            pltpu.VMEM((width + 8 * HEADS, padded), F32),
            pltpu.VMEM((width, padded), F32),
            pltpu.VMEM((padded, 2 * width), BF),
            pltpu.VMEM((total, width), F32),
            pltpu.VMEM((total, width), F32),
            pltpu.SMEM((4, 32), jnp.int32),
        ],
        compiler_params=pltpu.CompilerParams(vmem_limit_bytes=63 << 20),
        name="layer",
    )(gfeat, gcode, out_cot, bases_cot.T, row_weights, down_weights, vectors, table)

    me = lax.axis_index("eig")
    da_own = lax.dynamic_slice_in_dim(da_part, me, 1, 0)
    lead = (n - 1 if n > 1 else 1) + 1
    like = lambda a: shape(a.shape, F32)
    results = pl.pallas_call(
        functools.partial(finish_kernel, n, reach, grp_count),
        out_shape=[shape((tok, width), F32)]
        + [like(row_master)] * 3
        + [like(down_master)] * 3
        + [like(vectors)] * 3,
        in_specs=[ANY] + [VMEM] * 17,
        out_specs=[VMEM] * 10,
        scratch_shapes=[
            pltpu.VMEM((2 * reach, width, tok), BF),
            pltpu.VMEM((grp_count, share, lanes), F32),
            pltpu.VMEM((grp_count, share, 2 * width), F32),
            pltpu.VMEM((grp_count, share, 2 * width), F32),
            pltpu.VMEM((share, lanes), F32),
            pltpu.VMEM((n, share, lanes), F32),
            pltpu.VMEM((share, 2 * width), F32),
            pltpu.VMEM((n, share, 2 * width), F32),
            dma((2 * reach,)), dma((2 * reach,)),
            dma((grp_count,)), dma((grp_count,)),
            dma((grp_count,)), dma((grp_count,)),
            dma((n,)), dma((n,)),
            dma((n,)), dma((n,)),
        ],
        compiler_params=pltpu.CompilerParams(
            collective_id=1, has_side_effects=True, vmem_limit_bytes=48 << 20
        ),
        name="finish",
    )(
        da_part, da_own, features, eig_row, graph_ids, dh2, row_weights, vectors, table, grads,
        row_master, row_first, row_second, down_master, down_first, down_second,
        vec_first, vec_second,
    )
    return (out, bases.T, *results)


def solution(mesh):
    in_specs = (
        P(("grp", "eig"), None),
        P(("grp", "eig")),
        P("grp", "eig"),
        P(("grp", "eig"), None),
        P(("grp", "eig"), None),
        P(),
        P(),
        P(),
        P("grp", None),
        P("grp", None),
        P("grp", None),
        P("grp", None),
        P("grp", None),
        P("grp", None),
        P(),
        P(),
    )
    out_specs = (
        P(("grp", "eig"), None),
        P(("grp", "eig"), None),
        P(("grp", "eig"), None),
        P("grp", None),
        P("grp", None),
        P("grp", None),
        P("grp", None),
        P("grp", None),
        P("grp", None),
        P(),
        P(),
        P(),
    )
    return jax.shard_map(
        functools.partial(per_device, mesh.shape["eig"], mesh.shape["grp"]),
        mesh=mesh,
        in_specs=in_specs,
        out_specs=out_specs,
        check_vma=False,
    )
```
